256 devices in a mesh: src: 64 (over z, y_hi, x), row: 4 (over y_lo, core).
Axes of the slice: x: 4, y: 4 (y_hi: 2, y_lo: 2; y = y_hi * 2 + y_lo), z: 8, core: 2. Of those that a mesh axis runs over, the one named last changes fastest.
Arguments:
- factor: float32 [10240, 1024], P(('row', 'src')), as said below
- right_side: float32 [10240, 32768], P('row', 'src'), may hold values from -6 to 6
Outputs:
- advanced: float32 [10240, 32768], P('row', 'src')
The draws below stay inside these ranges and needn't reach their ends.
Inputs may be any that keep to these rules, and one draw needn't show every extreme that they name: factor is zero where its column index exceeds its row index, and its entries where the two are equal lie between 1 and 2.
All inputs are finite; a program needn't handle non-finite values.
Results may differ from the reference program's by a relative error of at most 0.0001.
Values sent between devices are 32-bit elements; how exact they have to be, the bound alone decides.
A program may use at most 64 MiB of HBM per device.

```python
import jax
import jax.numpy as jnp
from jax import lax

PB = 512
ROWS = 10240
RHS = 32768


def draw_factor(key, part):
    key_off = jax.random.fold_in(key, 11)
    key_diag = jax.random.fold_in(key, 23)
    shape = (ROWS, 2 * PB)
    spread = jax.random.normal(key_off, shape, jnp.float32)
    offdiag = spread * (0.4 / PB ** 0.5)
    diagval = jax.random.uniform(key_diag, shape, jnp.float32, 1.0, 2.0)
    row_ids = jnp.arange(ROWS)[:, None]
    col_ids = jnp.arange(2 * PB)[None, :]
    result = jnp.where(col_ids > row_ids, 0.0, jnp.where(col_ids == row_ids, diagval, offdiag))
    return result.astype(jnp.float32)


def level_of(own_key, extent, split, least, largest):
    level = 1.0
    for position, blocks in split:
        heights = jax.random.uniform(jax.random.fold_in(jax.random.fold_in(own_key, 6), position), (blocks,), jnp.float32, least / len(split), largest / len(split))
        level = level * jnp.repeat(jnp.exp(heights), extent[position] // blocks).reshape((-1,) + (1,) * (len(extent) - 1 - position))
    return level


def noise(own_key, shape, width, bound, split=(), held_as=jnp.bfloat16):
    drawn = width * jax.random.normal(own_key, shape, jnp.float32)
    if split:
        drawn = drawn * level_of(own_key, shape, split, -0.22, 0.18)
    return jnp.clip(drawn, -bound, bound).astype(held_as)


def setup_inputs(seed: int = 0) -> dict:
    key_list = jax.random.split(jax.random.key(seed), 3)
    factor = draw_factor(jax.random.fold_in(key_list[2], 71), 0)
    right_side = noise(key_list[1], (ROWS, RHS), 1.0, 6.0, ((0, 4), (1, 64)), jnp.float32)
    return dict(factor=factor, right_side=right_side)


def reference(factor, right_side):
    current = right_side
    for section in range(2):
        offset = section * PB
        diag_block = factor[offset:offset + PB, offset:offset + PB]
        solved = lax.linalg.triangular_solve(diag_block, current[offset:offset + PB], left_side=True, lower=True)
        below = factor[offset + PB:, offset:offset + PB]
        product = jnp.dot(below.astype(jnp.float32), solved.astype(jnp.float32), preferred_element_type=jnp.float32, precision=lax.Precision.HIGHEST)
        current = current.at[offset + PB:].set(current[offset + PB:] - product)
        current = current.at[offset:offset + PB].set(solved)
    return current
```

```python
import heapq

import jax
import jax.numpy as jnp
from jax import lax
from jax.experimental import pallas as pl
from jax.experimental.pallas import tpu as pltpu
from jax.sharding import PartitionSpec as P

MESH = pl.DeviceIdType.MESH

SB = 4096 * 8
def plan(A=2, NB=5, rate=46.5e3, lat=1.7, ylat=2.6, yrate=23e3, verbose=False):
    szA, szB = A * SB, (NB - A) * SB
    size = {"Y": NB * SB, "B1": szB, "B3": szB, "A1": szA, "A3": 4 * szA}
    nexthop = []
    free = {k: 0.0 for k in ("x+", "x-", "z+", "z-", "y")}
    busy = dict.fromkeys(free, 0.0)
    heap, order, cnt = [], [], 0
    sends = []
    def send(t, link, tag):
        nonlocal cnt
        r = yrate if link == "y" else rate
        s = max(t, free[link]); e = s + size[tag[0]] / r
        free[link] = e; busy[link] += size[tag[0]] / r
        sends.append((t, s, link, tag))
        heapq.heappush(heap, (e + (ylat if link == "y" else lat), cnt, link, tag)); cnt += 1
        order.append(("send", link, tag))
    def own(t, dh):
        for l in ("z+", "z-"): send(t, l, ("B1", 0, dh, 0))
        for l in ("x+", "x-"): send(t, l, ("A1", 0, dh, 0))
        for l in ("x+", "x-"): send(t, l, ("B3", 0, dh, 0))
    send(0, "y", ("Y", 0, 0, 0)); own(0, 0)
    got = {0: 0, 1: 0}
    T = 0
    arr = []
    while heap:
        t, _, link, tag = heapq.heappop(heap)
        k, dz, dh, dx = tag
        s = {"+": 1, "-": -1}.get(link[-1], 0)
        order.append(("recv", link, tag)); T = t; arr.append((t, link, tag))
        if k == "Y": own(t, 1); continue
        if link[0] == "x": dx -= s
        else: dz -= s
        if k in ("B1", "A3"):
            d = abs(dz)
            if d + 1 <= 3 or (d + 1 == 4 and (dh == 0) == (s == 1)):
                send(t, link, (k, dz, dh, dx))
            if k == "B1":
                for l in ("x+", "x-"): send(t, l, ("B3", dz, dh, 0))
        else:
            if abs(dx) == 1 and (dh == 0) == (s == 1):
                send(t, link, (k, dz, dh, dx))
            if k == "A1":
                got[dh] += 1
                if got[dh] == 3:
                    for l in ("z+", "z-"): send(t, l, ("A3", 0, dh, 0))
    if verbose:
        print("end", T, busy, "nsend", len(sends))
        for a in arr: print(a)
    return order, T


def make(A=2, NB=5, order=None, space=pl.ANY):
    if order is None:
        order, _ = plan(A, NB)
    RA = 8 * A
    RN = 8 * NB
    sends = [o for o in order if o[0] == "send"]
    idx = {(o[1], o[2]): i for i, o in enumerate(sends)}
    n = len(sends)
    def kernel(f_ref, g_ref, ssem, rsem, lsem):
        src = lax.axis_index("src"); row = lax.axis_index("row")
        z = src // 8; h = lax.rem(src // 4, 2); x = lax.rem(src, 4)
        def dev(dz=0, dh=0, dx=0):
            zz = lax.rem(z + dz + 8, 8); xx = lax.rem(x + dx + 4, 4)
            hh = h if not dh else 1 - h
            return (zz * 8 + hh * 4 + xx, row)
        nb = {"x+": dev(dx=1), "x-": dev(dx=-1), "z+": dev(dz=1), "z-": dev(dz=-1), "y": dev(dh=1)}
        bar = pltpu.get_barrier_semaphore()
        for k in nb.values():
            pl.semaphore_signal(bar, inc=1, device_id=k, device_id_type=MESH)
        loc = pltpu.make_async_copy(f_ref, g_ref.at[z, h, x], lsem)
        loc.start()
        pl.semaphore_wait(bar, len(nb))
        def ref(tag, own=True):
            k, dz, dh, dx = tag
            rows = {"Y": (0, RN), "B1": (RA, RN), "B3": (RA, RN), "A1": (0, RA), "A3": (0, RA)}[k]
            rs = pl.ds(rows[0], rows[1] - rows[0])
            if own and dz == 0 and dh == 0 and dx == 0 and k != "A3":
                s = f_ref.at[rs]
            else:
                s = None
            zz = lax.rem(z + dz + 8, 8); hh = h if not dh else 1 - h
            if k == "A3":
                g = g_ref.at[zz, hh, :, rs]
            else:
                g = g_ref.at[zz, hh, lax.rem(x + dx + 4, 4), rs]
            return (s if s is not None else g), g
        def desc(link, tag, shift):
            k, dz, dh, dx = tag
            if shift:
                s = {"+": 1, "-": -1}.get(link[-1], 0)
                t = (k, dz - s if link[0] == "z" else dz, 1 - dh if link == "y" else dh, dx - s if link[0] == "x" else dx)
                _, a = ref(t, own=False)
                b = a
            else:
                a, b = ref(tag)
            i = idx[(link, tag)]
            return pltpu.make_async_remote_copy(src_ref=a, dst_ref=b, send_sem=ssem.at[i], recv_sem=rsem.at[i], device_id=nb[link], device_id_type=MESH)
        waited = False
        for op, link, tag in order:
            if op == "send":
                if tag[0] == "A3" and not waited:
                    loc.wait(); waited = True
                desc(link, tag, False).start()
            else:
                desc(link, tag, True).wait_recv()
        for _, link, tag in sends:
            desc(link, tag, False).wait_send()
    def gather(f):
        return pl.pallas_call(
            kernel,
            out_shape=jax.ShapeDtypeStruct((8, 2, 4, RN, 1024), jnp.float32),
            in_specs=[pl.BlockSpec(memory_space=pltpu.VMEM)],
            out_specs=pl.BlockSpec(memory_space=space),
            scratch_shapes=[pltpu.SemaphoreType.DMA((n,)), pltpu.SemaphoreType.DMA((n,)), pltpu.SemaphoreType.DMA],
            compiler_params=pltpu.CompilerParams(collective_id=0, has_side_effects=True),
        )(f)
    return gather


def broadcast(block, axis, holder):
    block = jnp.where(lax.axis_index(axis) == holder, block, jnp.zeros_like(block))
    return lax.psum(block, axis)


def spread_solved(solved):
    return broadcast(solved, "row", 0)


def advance_panel(panel, current, offset, width, start_row):
    diag_block = panel[offset : offset + width]
    solved = lax.linalg.triangular_solve(
        diag_block, current[offset : offset + width], left_side=True, lower=True
    )
    solved = spread_solved(solved)
    product = jnp.dot(
        panel, solved, preferred_element_type=jnp.float32, precision=lax.Precision.HIGHEST
    )
    row_ids = start_row + jnp.arange(current.shape[0], dtype=jnp.int32)[:, None]
    updated = jnp.where(row_ids >= offset + width, current - product, current)
    holder = row_ids[offset : offset + width] < offset + width
    placed = jnp.where(holder, solved, updated[offset : offset + width])
    return lax.dynamic_update_slice_in_dim(updated, placed, offset, 0)


def local(factor, right_side):
    width = factor.shape[1] // 2
    local_rows = right_side.shape[0]
    start_row = lax.axis_index("row") * local_rows
    current = right_side
    gathered = make()(factor).reshape(local_rows, factor.shape[1])
    first_panel = gathered[:, :width]
    second_panel = gathered[:, width:]
    current = advance_panel(first_panel, current, 0, width, start_row)
    current = advance_panel(second_panel, current, width, width, start_row)
    return current


def solution(mesh):
    placed = (P(("row", "src"), None), P("row", "src"))
    return jax.shard_map(
        local, mesh=mesh, in_specs=placed, out_specs=P("row", "src"), check_vma=False
    )
```

```python
import heapq

import jax
import jax.numpy as jnp
from jax import lax
from jax.experimental import pallas as pl
from jax.experimental.pallas import tpu as pltpu
from jax.sharding import PartitionSpec as P

MESH = pl.DeviceIdType.MESH
NX, NH, NZ = 4, 2, 8
PIECE = 40
COLS = 1024
WIDTH = 512
BLK = 128
STEPS = COLS // BLK
RATE = {"x+": 46e3, "x-": 46e3, "z+": 75e3, "z-": 75e3, "y": 23e3}


def plan(rows_a, latency=1.7):
    size = {"Y": PIECE, "B1": PIECE - rows_a, "B3": PIECE - rows_a, "A1": rows_a, "A3": 4 * rows_a}
    free = dict.fromkeys(RATE, 0.0)
    heap, order = [], []

    def send(t, link, tag):
        end = max(t, free[link]) + size[tag[0]] * 4096 / RATE[link]
        free[link] = end
        heapq.heappush(heap, (end + latency, len(order), link, tag))
        order.append(("send", link, tag))

    def own(t, dh):
        for link in ("x+", "x-"):
            send(t, link, ("A1", 0, dh, 0))
        for link in ("z+", "z-"):
            send(t, link, ("B1", 0, dh, 0))
        for link in ("x+", "x-"):
            send(t, link, ("B3", 0, dh, 0))

    send(0, "y", ("Y", 0, 0, 0))
    own(0, 0)
    got = {0: 0, 1: 0}
    while heap:
        t, _, link, tag = heapq.heappop(heap)
        kind, dz, dh, dx = tag
        step = {"+": 1, "-": -1}.get(link[-1], 0)
        order.append(("recv", link, tag))
        if kind == "Y":
            own(t, 1)
            continue
        if link[0] == "x":
            dx -= step
        else:
            dz -= step
        if kind in ("B1", "A3"):
            far = abs(dz) + 1
            if far <= 3 or (far == 4 and (dh == 0) == (step == 1)):
                send(t, link, (kind, dz, dh, dx))
            if kind == "B1":
                for side in ("x+", "x-"):
                    send(t, side, ("B3", dz, dh, 0))
        else:
            if abs(dx) == 1 and (dh == 0) == (step == 1):
                send(t, link, (kind, dz, dh, dx))
            if kind == "A1":
                got[dh] += 1
                if got[dh] == 3:
                    for side in ("z+", "z-"):
                        send(t, side, ("A3", 0, dh, 0))
    return order


ROWS_A = 32
ORDER = plan(ROWS_A)
SENDS = [op for op in ORDER if op[0] == "send"]
SEND_INDEX = {(op[1], op[2]): i for i, op in enumerate(SENDS)}
NSEM = len(SENDS)


def visiting_order():
    table = []
    for z in range(NZ):
        dist = lambda b: min((b - z) % NZ, (z - b) % NZ)
        top = sorted((b for b in range(4) if b != z), key=dist)
        rest = sorted((b for b in range(4, NZ) if b != z), key=dist)
        table.append([z] + top + rest)
    return [sum(table[z][k] * NZ**z for z in range(NZ)) for k in range(NZ)]


VISIT = visiting_order()


def split(a):
    hi = a.astype(jnp.bfloat16)
    lo = (a - hi.astype(jnp.float32)).astype(jnp.bfloat16)
    return hi, lo


def dot3(a, b):
    ah, al = split(a)
    bh, bl = split(b)
    d = lambda p, q: jnp.dot(p, q, preferred_element_type=jnp.float32)
    return d(ah, bh) + (d(ah, bl) + d(al, bh))


def gather_solve(f_ref, r_ref, g_ref, x_ref, top, cur, inv, ssem, rsem, xs, xr, lsem):
    src = lax.axis_index("src")
    row = lax.axis_index("row")
    z, h, x = src // (NH * NX), lax.rem(src // NX, NH), lax.rem(src, NX)
    core, y_lo = lax.rem(row, 2), row // 2

    def dev(dz=0, flip=False, dx=0):
        zz = lax.rem(z + dz + NZ, NZ)
        hh = 1 - h if flip else h
        return (zz * (NH * NX) + hh * NX + lax.rem(x + dx + NX, NX), row)

    link_to = {"x+": dev(dx=1), "x-": dev(dx=-1), "z+": dev(dz=1), "z-": dev(dz=-1), "y": dev(flip=True)}
    barrier = pltpu.get_barrier_semaphore()
    friends = list(link_to.values()) + [(src, lax.rem(row + i, 4)) for i in (1, 2, 3)]
    for friend in friends:
        pl.semaphore_signal(barrier, inc=1, device_id=friend, device_id_type=MESH)
    keep = pltpu.make_async_copy(f_ref, g_ref.at[z, h, x], lsem.at[0])
    keep.start()
    fetch = pltpu.make_async_copy(r_ref.at[pl.ds(0, COLS)], cur, lsem.at[1])
    solver = jnp.logical_and(core == 0, y_lo == 0)

    @pl.when(solver)
    def _():
        fetch.start()

    pl.semaphore_wait(barrier, len(friends))

    def remote(a, b, s, r, to):
        return pltpu.make_async_remote_copy(
            src_ref=a, dst_ref=b, send_sem=s, recv_sem=r, device_id=to, device_id_type=MESH
        )

    def xblock(ref, j):
        return ref.at[pl.ds(j * BLK, BLK)]

    def x_send(j, k, local=True):
        to = (src, k)
        i = j + STEPS * (0 if k == 2 or k == 3 else 1)
        return remote(xblock(cur if local else x_ref, j), xblock(x_ref, j), xs.at[i], xr.at[j], to)

    SY, SOWN, SZ, SX = 0, 1, 5, 21
    RY, RZ, RX = 0, 1, 17

    @pl.when(core == 0)
    def _():
        piece = lambda zz, dh, xx: g_ref.at[zz, h if dh == 0 else 1 - h, xx]
        zs = [lax.rem(lax.shift_right_logical(jnp.int32(VISIT[k]), 3 * z), NZ) for k in range(NZ)]
        me = f_ref
        xl, xr_ = lax.rem(x + 3, NX), lax.rem(x + 1, NX)
        x2 = lax.rem(x + 2, NX)

        def y_copy():
            return remote(me, piece(z, 0, x), ssem.at[SY], rsem.at[RY], link_to["y"])

        def own_z(dh, side):
            a = me if dh == 0 else piece(z, 1, x)
            return remote(a, piece(z, dh, x), ssem.at[SOWN + 2 * dh + (side == "z-")], rsem.at[RZ + z * 2 + dh], link_to[side])

        def z_copy(k, dh):
            b = zs[k]
            d = lax.rem(z - b + NZ, NZ)
            tz = lax.rem(z + 1 - 2 * (d // 4) + NZ, NZ)
            go = jnp.logical_or(d <= 3 - dh, d >= 6 - dh)
            i = b * 2 + dh
            return go, remote(
                piece(b, dh, x), piece(b, dh, x), ssem.at[SZ + i], rsem.at[RZ + i],
                (tz * (NH * NX) + h * NX + x, row),
            )

        def x_copy(k, dh, which):
            b = zs[k]
            i = (b * 2 + dh) * 3 + which
            if which == 2:
                at = xl if dh == 0 else xr_
                to = link_to["x+"] if dh == 0 else link_to["x-"]
                a = piece(b, dh, at)
                return remote(a, a, ssem.at[SX + i], rsem.at[RX + i], to)
            a = me if k == 0 and dh == 0 else piece(b, dh, x)
            return remote(a, piece(b, dh, x), ssem.at[SX + i], rsem.at[RX + i], link_to["x+" if which == 0 else "x-"])

        def x_arrive(k, dh, which):
            b = zs[k]
            i = (b * 2 + dh) * 3 + which
            at = (xl, xr_, x2)[which]
            a = piece(b, dh, at)
            remote(a, a, ssem.at[SX + i], rsem.at[RX + i], link_to["x+"]).wait_recv()

        def z_part(k):
            for dh in (0, 1):
                go, c = z_copy(k, dh)
                c.wait_recv()
                pl.when(go)(c.start)

        def x_part(k):
            for dh in (0, 1):
                x_copy(k, dh, 0).start()
                x_copy(k, dh, 1).start()

        def x_on(k):
            x_arrive(k, 0, 0)
            x_copy(k, 0, 2).start()
            x_arrive(k, 1, 1)
            x_copy(k, 1, 2).start()

        def x_rest(k):
            x_arrive(k, 0, 1)
            x_arrive(k, 1, 0)
            x_arrive(k, 0, 2)
            x_arrive(k, 1, 2)

        y_copy().start()
        for side in ("z+", "z-"):
            own_z(0, side).start()
        x_copy(0, 0, 0).start()
        x_copy(0, 0, 1).start()
        remote(piece(z, 1, x), piece(z, 1, x), ssem.at[SY], rsem.at[RY], link_to["y"]).wait_recv()
        for side in ("z+", "z-"):
            own_z(1, side).start()
        x_copy(0, 1, 0).start()
        x_copy(0, 1, 1).start()
        for k in (1, 2, 3, 4):
            z_part(k)
            x_part(k)
            x_on(k - 1)
            if k >= 3:
                z_part(k + 2)
        x_on(4)
        z_part(7)
        for k in (5, 6, 7):
            x_part(k)
        for k in range(5):
            x_rest(k)

        @pl.when(y_lo == 0)
        def _():
            keep.wait()
            rows = NH * NX * PIECE
            loads = []
            for b in range(4):
                n = min(rows, COLS - b * rows)
                for q in range(0, n, PIECE):
                    hh, xx = q // (NX * PIECE), (q // PIECE) % NX
                    m = min(PIECE, n - q)
                    loads.append(pltpu.make_async_copy(
                        g_ref.at[b, hh, xx, pl.ds(0, m)], top.at[pl.ds(b * rows + q, m)], lsem.at[2 + len(loads)]))
            for c in loads:
                c.start()
            for c in loads:
                c.wait()
            fetch.wait()
            ii = lax.broadcasted_iota(jnp.int32, (BLK, BLK), 0)
            jj = lax.broadcasted_iota(jnp.int32, (BLK, BLK), 1)
            for j in range(STEPS):
                a = top[pl.ds(j * BLK, BLK), pl.ds(j * BLK, BLK)]
                dg = jnp.where(ii == jj, a, 0.0)
                dc = 1.0 / jnp.sum(dg, axis=1, keepdims=True)
                dr = 1.0 / jnp.sum(dg, axis=0, keepdims=True)
                pair = jnp.logical_and(ii == jj + 1, lax.rem(ii, 2) == 1)
                inv[j] = jnp.where(ii == jj, dc, jnp.where(pair, -(dc * a) * dr, 0.0))

            def level(t, carry):
                bi, bj = lax.shift_right_logical(ii, t), lax.shift_right_logical(jj, t)
                below = jnp.logical_and(bi == bj + 1, lax.rem(bi, 2) == 1)
                for j in range(STEPS):
                    a = top[pl.ds(j * BLK, BLK), pl.ds(j * BLK, BLK)]
                    v = inv[j]
                    inv[j] = v - dot3(v, dot3(jnp.where(below, a, 0.0), v))
                return carry

            lax.fori_loop(1, 7, level, 0)
            x_on(5)
            for j in range(STEPS):
                solved = dot3(inv[j], cur[pl.ds(j * BLK, BLK)])
                cur[pl.ds(j * BLK, BLK)] = solved
                left = COLS - (j + 1) * BLK
                if left:
                    below = pl.ds((j + 1) * BLK, left)
                    cur[below] = cur[below] - dot3(top[below, pl.ds(j * BLK, BLK)], solved)
                if j >= 1:
                    x_send(j - 1, 2).start()
                    x_send(j - 1, 1).start()
                if j == 1:
                    x_on(6)
                if j == 3:
                    x_on(7)
            store = pltpu.make_async_copy(cur, x_ref, lsem.at[2])
            store.start()
            x_send(STEPS - 1, 2).start()
            x_send(STEPS - 1, 1).start()
            store.wait()
            for j in range(STEPS):
                x_send(j, 2).wait_send()
                x_send(j, 1).wait_send()

        @pl.when(y_lo == 1)
        def _():
            keep.wait()
            x_on(5)
            for j in range(STEPS):
                x_send(j, 3, local=False).wait_recv()
                x_send(j, 3, local=False).start()
                if j == 1:
                    x_on(6)
                if j == 3:
                    x_on(7)
            for j in range(STEPS):
                x_send(j, 3, local=False).wait_send()

        for k in (5, 6, 7):
            x_rest(k)
        y_copy().wait_send()
        for dh in (0, 1):
            for side in ("z+", "z-"):
                own_z(dh, side).wait_send()
            for k in range(NZ):
                if k:
                    go, c = z_copy(k, dh)
                    pl.when(go)(c.wait_send)
                for which in range(3):
                    x_copy(k, dh, which).wait_send()

    @pl.when(core == 1)
    def _():
        def at(tag, own):
            kind, dz, dh, dx = tag
            first, n = {"Y": (0, PIECE), "B1": (ROWS_A, PIECE - ROWS_A), "B3": (ROWS_A, PIECE - ROWS_A),
                        "A1": (0, ROWS_A), "A3": (0, ROWS_A)}[kind]
            rows = pl.ds(first, n)
            zz, hh = lax.rem(z + dz + NZ, NZ), h if dh == 0 else 1 - h
            if kind == "A3":
                g = g_ref.at[zz, hh, :, rows]
            else:
                g = g_ref.at[zz, hh, lax.rem(x + dx + NX, NX), rows]
            if own and dz == 0 and dh == 0 and dx == 0 and kind != "A3":
                return f_ref.at[rows], g
            return g, g

        def sent(link, tag):
            a, b = at(tag, True)
            i = SEND_INDEX[(link, tag)]
            return remote(a, b, ssem.at[i], rsem.at[i], link_to[link])

        def arriving(link, tag):
            kind, dz, dh, dx = tag
            step = {"+": 1, "-": -1}.get(link[-1], 0)
            if link[0] == "z":
                dz -= step
            elif link[0] == "x":
                dx -= step
            else:
                dh = 1 - dh
            _, b = at((kind, dz, dh, dx), False)
            i = SEND_INDEX[(link, tag)]
            return remote(b, b, ssem.at[i], rsem.at[i], link_to[link])

        kept = False
        for op, link, tag in ORDER:
            if op == "send":
                if tag[0] == "A3" and not kept:
                    keep.wait()
                    kept = True
                sent(link, tag).start()
            else:
                arriving(link, tag).wait_recv()
        for _, link, tag in SENDS:
            sent(link, tag).wait_send()
        for j in range(STEPS):
            x_send(j, 3, local=False).wait_recv()


TILE = 512


def update(f_ref, x_ref, r_ref, o_ref, xh, xl):
    i = pl.program_id(0)
    row = lax.axis_index("row")

    @pl.when(i == 0)
    def _():
        hi, lo = split(x_ref[...])
        xh[...] = hi
        xl[...] = lo

    solved = jnp.logical_and(row == 0, i < COLS // TILE)

    @pl.when(solved)
    def _():
        o_ref[...] = x_ref[pl.ds(pl.multiple_of(lax.rem(i, COLS // TILE) * TILE, TILE), TILE)]

    @pl.when(jnp.logical_not(solved))
    def _():
        fh, fl = split(f_ref[...])
        d = lambda p, q: jnp.dot(p, q[...], preferred_element_type=jnp.float32)
        o_ref[...] = r_ref[...] - (d(fh, xh) + (d(fh, xl) + d(fl, xh)))


def local(factor, right_side):
    rows, width = right_side.shape
    ANY = pl.BlockSpec(memory_space=pl.ANY)
    gathered, solved = pl.pallas_call(
        gather_solve,
        out_shape=(
            jax.ShapeDtypeStruct((NZ, NH, NX, PIECE, COLS), jnp.float32),
            jax.ShapeDtypeStruct((COLS, width), jnp.float32),
        ),
        in_specs=[pl.BlockSpec(memory_space=pltpu.VMEM), ANY],
        out_specs=(ANY, ANY),
        scratch_shapes=[
            pltpu.VMEM((COLS, COLS), jnp.float32),
            pltpu.VMEM((COLS, width), jnp.float32),
            pltpu.VMEM((STEPS, BLK, BLK), jnp.float32),
            pltpu.SemaphoreType.DMA((NSEM,)),
            pltpu.SemaphoreType.DMA((NSEM,)),
            pltpu.SemaphoreType.DMA((2 * STEPS,)),
            pltpu.SemaphoreType.DMA((STEPS,)),
            pltpu.SemaphoreType.DMA((32,)),
        ],
        compiler_params=pltpu.CompilerParams(collective_id=0, has_side_effects=True),
    )(factor, right_side)
    return pl.pallas_call(
        update,
        grid=(rows // TILE,),
        out_shape=jax.ShapeDtypeStruct((rows, width), jnp.float32),
        in_specs=[
            pl.BlockSpec((TILE, COLS), lambda i: (i, 0)),
            pl.BlockSpec((COLS, width), lambda i: (0, 0)),
            pl.BlockSpec((TILE, width), lambda i: (i, 0)),
        ],
        out_specs=pl.BlockSpec((TILE, width), lambda i: (i, 0)),
        scratch_shapes=[pltpu.VMEM((COLS, width), jnp.bfloat16), pltpu.VMEM((COLS, width), jnp.bfloat16)],
    )(gathered.reshape(rows, COLS), solved, right_side)


def solution(mesh):
    placed = (P(("row", "src"), None), P("row", "src"))
    return jax.shard_map(
        local, mesh=mesh, in_specs=placed, out_specs=P("row", "src"), check_vma=False
    )
```

```python
import heapq

import jax
import jax.numpy as jnp
from jax import lax
from jax.experimental import pallas as pl
from jax.experimental.pallas import tpu as pltpu
from jax.sharding import PartitionSpec as P

MESH = pl.DeviceIdType.MESH
NX, NH, NZ = 4, 2, 8
PIECE = 40
COLS = 1024
WIDTH = 512
BLK = 128
STEPS = COLS // BLK
PIECES = -(-COLS // PIECE)
BANDS = -(-PIECES // NX)
UNITS = PIECES + BANDS
TOPZ = -(-PIECES // (NX * NH))
CHUNKS = 4
RATE = {"x+": 46e3, "x-": 46e3, "z+": 46e3, "z-": 46e3, "y": 23e3}


def plan(rows_a, latency=1.7):
    size = {"Y": PIECE, "B1": PIECE - rows_a, "B3": PIECE - rows_a, "A1": rows_a, "A3": 4 * rows_a}
    free = dict.fromkeys(RATE, 0.0)
    heap, order = [], []

    def send(t, link, tag):
        end = max(t, free[link]) + size[tag[0]] * 4096 / RATE[link]
        free[link] = end
        heapq.heappush(heap, (end + latency, len(order), link, tag))
        order.append(("send", link, tag))

    def own(t, dh):
        for link in ("z+", "z-"):
            send(t, link, ("B1", 0, dh, 0))
        for link in ("x+", "x-"):
            send(t, link, ("A1", 0, dh, 0))
        for link in ("x+", "x-"):
            send(t, link, ("B3", 0, dh, 0))

    send(0, "y", ("Y", 0, 0, 0))
    own(0, 0)
    got = {0: 0, 1: 0}
    while heap:
        t, _, link, tag = heapq.heappop(heap)
        kind, dz, dh, dx = tag
        step = {"+": 1, "-": -1}.get(link[-1], 0)
        order.append(("recv", link, tag))
        if kind == "Y":
            own(t, 1)
            continue
        if link[0] == "x":
            dx -= step
        else:
            dz -= step
        if kind in ("B1", "A3"):
            far = abs(dz) + 1
            if far <= 3 or (far == 4 and (dh == 0) == (step == 1)):
                send(t, link, (kind, dz, dh, dx))
            if kind == "B1":
                for side in ("x+", "x-"):
                    send(t, side, ("B3", dz, dh, 0))
        else:
            if abs(dx) == 1 and (dh == 0) == (step == 1):
                send(t, link, (kind, dz, dh, dx))
            if kind == "A1":
                got[dh] += 1
                if got[dh] == 3:
                    for side in ("z+", "z-"):
                        send(t, side, ("A3", 0, dh, 0))
    return order


ROWS_A = 16
ORDER = plan(ROWS_A)
SENDS = [op for op in ORDER if op[0] == "send"]
SEND_INDEX = {(op[1], op[2]): i for i, op in enumerate(SENDS)}
NSEM = len(SENDS)


def split(a):
    hi = a.astype(jnp.bfloat16)
    lo = (a - hi.astype(jnp.float32)).astype(jnp.bfloat16)
    return hi, lo


def dot3(a, b):
    ah, al = split(a)
    bh, bl = split(b)
    d = lambda p, q: jnp.dot(p, q, preferred_element_type=jnp.float32)
    return d(ah, bh) + (d(ah, bl) + d(al, bh))


def gather_solve(f_ref, r_ref, g_ref, x_ref, t_ref, top, cur, inv, ssem, rsem, xs, xr, ts, tr, lsem):
    src = lax.axis_index("src")
    row = lax.axis_index("row")
    z, h, x = src // (NH * NX), lax.rem(src // NX, NH), lax.rem(src, NX)
    core, y_lo = lax.rem(row, 2), row // 2

    def dev(dz=0, flip=False, dx=0):
        zz = lax.rem(z + dz + NZ, NZ)
        hh = 1 - h if flip else h
        return (zz * (NH * NX) + hh * NX + lax.rem(x + dx + NX, NX), row)

    link_to = {"x+": dev(dx=1), "x-": dev(dx=-1), "z+": dev(dz=1), "z-": dev(dz=-1), "y": dev(flip=True)}
    beside = (src, row + 1 - 2 * core)
    across = ((src, lax.rem(row + 2, 4)), (dev(flip=True)[0], lax.rem(row + 2, 4)))
    barrier = pltpu.get_barrier_semaphore()
    friends = list(link_to.values()) + [beside, *across]
    for friend in friends:
        pl.semaphore_signal(barrier, inc=1, device_id=friend, device_id_type=MESH)
    keep = pltpu.make_async_copy(f_ref, g_ref.at[z, h, x], lsem.at[0])
    keep.start()
    fetch = pltpu.make_async_copy(r_ref.at[pl.ds(0, COLS)], cur, lsem.at[1])
    first = jnp.logical_and(core == 0, y_lo == 0)
    pl.when(first)(fetch.start)
    pl.semaphore_wait(barrier, len(friends))

    def remote(a, b, s, r, to):
        return pltpu.make_async_remote_copy(
            src_ref=a, dst_ref=b, send_sem=s, recv_sem=r, device_id=to, device_id_type=MESH
        )

    ROWS = {"Y": (0, PIECE), "B1": (ROWS_A, PIECE - ROWS_A), "B3": (ROWS_A, PIECE - ROWS_A),
            "A1": (0, ROWS_A), "A3": (0, ROWS_A)}

    def where(tag):
        kind, dz, dh, dx = tag
        rows = pl.ds(*ROWS[kind])
        zz, hh = lax.rem(z + dz + NZ, NZ), h if dh == 0 else 1 - h
        return (zz, hh, slice(None), rows) if kind == "A3" else (zz, hh, lax.rem(x + dx + NX, NX), rows)

    def sent(i):
        _, link, tag = SENDS[i]
        b = g_ref.at[where(tag)]
        a = f_ref.at[pl.ds(*ROWS[tag[0]])] if tag[1:] == (0, 0, 0) and tag[0] != "A3" else b
        return remote(a, b, ssem.at[i], rsem.at[i], link_to[link])

    def landed(i):
        _, link, (kind, dz, dh, dx) = SENDS[i]
        step = {"+": 1, "-": -1}.get(link[-1], 0)
        if link[0] == "z":
            dz -= step
        elif link[0] == "x":
            dx -= step
        else:
            dh = 1 - dh
        return kind, dz, dh, dx

    handed = []

    def up(tag, half):
        kind, dz, dh, dx = tag
        zz, hh, xx, rows = where(tag)
        if kind == "A3":
            unit, count = zz * NH + hh, BANDS
            base = PIECES
        else:
            unit, count = (zz * NH + hh) * NX + xx, PIECES
            base = 0
        go = jnp.logical_and(first, unit < count)
        if half == 0:
            go = jnp.logical_and(go, zz >= 1)
        elif dh == 1:
            go = jnp.logical_and(go, zz == 0)
        i = base + lax.min(unit, count - 1)
        at = (lax.min(zz, TOPZ - 1), hh, xx, rows)
        a = f_ref.at[rows] if tag[1:] == (0, 0, 0) and kind != "A3" else g_ref.at[where(tag)]
        return go, remote(a, t_ref.at[at], ts.at[half * UNITS + i], tr.at[i], across[half])

    def hand_up(tag):
        for half in (0, 1) if tag[2] == 0 else (1,):
            go, c = up(tag, half)
            pl.when(go)(c.start)
            handed.append((tag, half))

    def right(i):
        rows = pl.ds(i * (COLS // CHUNKS), COLS // CHUNKS)
        return remote(r_ref.at[rows], cur.at[rows], ts.at[2 * UNITS + i], tr.at[UNITS + i], across[0])

    kept = False
    arrived = 0
    for op, link, tag in ORDER:
        i = SEND_INDEX[(link, tag)]
        if op == "send":
            if tag[0] == "A3" and not kept:
                keep.wait()
                kept = True
            sent(i).start()
            if link == "z+" and tag[1] == 0:
                hand_up(("A3", 0, tag[2], 0) if tag[0] == "A3" else ("B3", 0, tag[2], 0))
            continue
        got = landed(i)
        b = g_ref.at[where(got)]
        remote(b, b, ssem.at[i], rsem.at[i], link_to[link]).wait_recv()
        if got[0] in ("A3", "B3"):
            hand_up(got)
        elif got[0] == "B1":
            hand_up(("B3",) + got[1:])
        arrived += 1
        if arrived % 12 == 11 and arrived // 12 < CHUNKS:
            pl.when(first)(right(arrived // 12).start)

    def x_send(j):
        rows = pl.ds(j * BLK, BLK)
        return remote(cur.at[rows], x_ref.at[rows], xs.at[j], xr.at[j], beside)

    @pl.when(core == 0)
    def _():
        def load(ref):
            loads = []
            for p in range(PIECES):
                loads.append(pltpu.make_async_copy(
                    ref.at[p // (NH * NX), p // NX % NH, p % NX], top.at[pl.ds(p * PIECE, PIECE)], lsem.at[2 + p]))
            for c in loads:
                c.start()
            for c in loads:
                c.wait()

        @pl.when(y_lo == 0)
        def _():
            load(g_ref)
            fetch.wait()

        @pl.when(y_lo == 1)
        def _():
            for p in range(PIECES):
                a = t_ref.at[p // (NH * NX), p // NX % NH, p % NX, pl.ds(ROWS_A, PIECE - ROWS_A)]
                remote(a, a, ts.at[p], tr.at[p], across[0]).wait_recv()
            for u in range(BANDS):
                a = t_ref.at[u // NH, u % NH, :, pl.ds(0, ROWS_A)]
                remote(a, a, ts.at[PIECES + u], tr.at[PIECES + u], across[0]).wait_recv()
            load(t_ref)
            for i in range(CHUNKS):
                right(i).wait_recv()

        ii = lax.broadcasted_iota(jnp.int32, (BLK, BLK), 0)
        jj = lax.broadcasted_iota(jnp.int32, (BLK, BLK), 1)
        for j in range(STEPS):
            a = top[pl.ds(j * BLK, BLK), pl.ds(j * BLK, BLK)]
            dg = jnp.where(ii == jj, a, 0.0)
            dc = 1.0 / jnp.sum(dg, axis=1, keepdims=True)
            dr = 1.0 / jnp.sum(dg, axis=0, keepdims=True)
            pair = jnp.logical_and(ii == jj + 1, lax.rem(ii, 2) == 1)
            inv[j] = jnp.where(ii == jj, dc, jnp.where(pair, -(dc * a) * dr, 0.0))

        def level(t, carry):
            bi, bj = lax.shift_right_logical(ii, t), lax.shift_right_logical(jj, t)
            below = jnp.logical_and(bi == bj + 1, lax.rem(bi, 2) == 1)
            for j in range(STEPS):
                a = top[pl.ds(j * BLK, BLK), pl.ds(j * BLK, BLK)]
                v = inv[j]
                inv[j] = v - dot3(v, dot3(jnp.where(below, a, 0.0), v))
            return carry

        lax.fori_loop(1, 7, level, 0)
        for j in range(STEPS):
            rows = pl.ds(j * BLK, BLK)
            solved = dot3(inv[j], cur[rows])
            cur[rows] = solved
            left = COLS - (j + 1) * BLK
            if left:
                below = pl.ds((j + 1) * BLK, left)
                cur[below] = cur[below] - dot3(top[below, rows], solved)
            if j >= 1:
                x_send(j - 1).start()
        store = pltpu.make_async_copy(cur, x_ref, lsem.at[2])
        store.start()
        x_send(STEPS - 1).start()
        store.wait()
        for j in range(STEPS):
            x_send(j).wait_send()

    @pl.when(core == 1)
    def _():
        for j in range(STEPS):
            x_send(j).wait_recv()

    for i in range(NSEM):
        sent(i).wait_send()
    for tag, half in handed:
        go, c = up(tag, half)
        pl.when(go)(c.wait_send)

    @pl.when(first)
    def _():
        for i in range(CHUNKS):
            right(i).wait_send()


TILE = 512


def update(f_ref, x_ref, r_ref, o_ref, xh, xl):
    i = pl.program_id(0)
    row = lax.axis_index("row")

    @pl.when(i == 0)
    def _():
        hi, lo = split(x_ref[...])
        xh[...] = hi
        xl[...] = lo

    solved = jnp.logical_and(row == 0, i < COLS // TILE)

    @pl.when(solved)
    def _():
        o_ref[...] = x_ref[pl.ds(pl.multiple_of(lax.rem(i, COLS // TILE) * TILE, TILE), TILE)]

    @pl.when(jnp.logical_not(solved))
    def _():
        fh, fl = split(f_ref[...])
        d = lambda p, q: jnp.dot(p, q[...], preferred_element_type=jnp.float32)
        o_ref[...] = r_ref[...] - (d(fh, xh) + (d(fh, xl) + d(fl, xh)))


def local(factor, right_side):
    rows, width = right_side.shape
    ANY = pl.BlockSpec(memory_space=pl.ANY)
    gathered, solved, _ = pl.pallas_call(
        gather_solve,
        out_shape=(
            jax.ShapeDtypeStruct((NZ, NH, NX, PIECE, COLS), jnp.float32),
            jax.ShapeDtypeStruct((COLS, width), jnp.float32),
            jax.ShapeDtypeStruct((TOPZ, NH, NX, PIECE, COLS), jnp.float32),
        ),
        in_specs=[pl.BlockSpec(memory_space=pltpu.VMEM), ANY],
        out_specs=(ANY, ANY, ANY),
        scratch_shapes=[
            pltpu.VMEM((PIECES * PIECE, COLS), jnp.float32),
            pltpu.VMEM((COLS, width), jnp.float32),
            pltpu.VMEM((STEPS, BLK, BLK), jnp.float32),
            pltpu.SemaphoreType.DMA((NSEM,)),
            pltpu.SemaphoreType.DMA((NSEM,)),
            pltpu.SemaphoreType.DMA((STEPS,)),
            pltpu.SemaphoreType.DMA((STEPS,)),
            pltpu.SemaphoreType.DMA((2 * UNITS + CHUNKS,)),
            pltpu.SemaphoreType.DMA((UNITS + CHUNKS,)),
            pltpu.SemaphoreType.DMA((32,)),
        ],
        compiler_params=pltpu.CompilerParams(collective_id=0, has_side_effects=True),
    )(factor, right_side)
    return pl.pallas_call(
        update,
        grid=(rows // TILE,),
        out_shape=jax.ShapeDtypeStruct((rows, width), jnp.float32),
        in_specs=[
            pl.BlockSpec((TILE, COLS), lambda i: (i, 0)),
            pl.BlockSpec((COLS, width), lambda i: (0, 0)),
            pl.BlockSpec((TILE, width), lambda i: (i, 0)),
        ],
        out_specs=pl.BlockSpec((TILE, width), lambda i: (i, 0)),
        scratch_shapes=[pltpu.VMEM((COLS, width), jnp.bfloat16), pltpu.VMEM((COLS, width), jnp.bfloat16)],
    )(gathered.reshape(rows, COLS), solved, right_side)


def solution(mesh):
    placed = (P(("row", "src"), None), P("row", "src"))
    return jax.shard_map(
        local, mesh=mesh, in_specs=placed, out_specs=P("row", "src"), check_vma=False
    )
```

```python
import heapq

import jax
import jax.numpy as jnp
from jax import lax
from jax.experimental import pallas as pl
from jax.experimental.pallas import tpu as pltpu
from jax.sharding import PartitionSpec as P

MESH = pl.DeviceIdType.MESH
NX, NH, NZ = 4, 2, 8
PIECE = 40
COLS = 1024
WIDTH = 512
BLK = 128
STEPS = COLS // BLK
PIECES = -(-COLS // PIECE)
UNITS = 2 * PIECES
CHUNKS = 4
GATE = 32
RATE = {"x+": 46e3, "x-": 46e3, "z+": 46e3, "z-": 46e3, "y": 23e3}


def plan(rows_a, latency=1.7):
    size = {"Y": PIECE, "B1": PIECE - rows_a, "B3": PIECE - rows_a, "A1": rows_a, "A3": 4 * rows_a}
    free = dict.fromkeys(RATE, 0.0)
    heap, order = [], []

    def send(t, link, tag):
        end = max(t, free[link]) + size[tag[0]] * 4096 / RATE[link]
        free[link] = end
        heapq.heappush(heap, (end + latency, len(order), link, tag))
        order.append(("send", link, tag))

    def own(t, dh):
        for link in ("z+", "z-"):
            send(t, link, ("B1", 0, dh, 0))
        for link in ("x+", "x-"):
            send(t, link, ("A1", 0, dh, 0))
        for link in ("x+", "x-"):
            send(t, link, ("B3", 0, dh, 0))

    send(0, "y", ("Y", 0, 0, 0))
    own(0, 0)
    got = {0: 0, 1: 0}
    while heap:
        t, _, link, tag = heapq.heappop(heap)
        kind, dz, dh, dx = tag
        step = {"+": 1, "-": -1}.get(link[-1], 0)
        order.append(("recv", link, tag))
        if kind == "Y":
            own(t, 1)
            continue
        if link[0] == "x":
            dx -= step
        else:
            dz -= step
        if kind in ("B1", "A3"):
            far = abs(dz) + 1
            if far <= 3 or (far == 4 and (dh == 0) == (step == 1)):
                send(t, link, (kind, dz, dh, dx))
            if kind == "B1":
                for side in ("x+", "x-"):
                    send(t, side, ("B3", dz, dh, 0))
        else:
            if abs(dx) == 1 and (dh == 0) == (step == 1):
                send(t, link, (kind, dz, dh, dx))
            if kind == "A1":
                got[dh] += 1
                if got[dh] == 3:
                    for side in ("z+", "z-"):
                        send(t, side, ("A3", 0, dh, 0))
    return order


ROWS_A = 16
ORDER = plan(ROWS_A)
SENDS = [op for op in ORDER if op[0] == "send"]
SEND_INDEX = {(op[1], op[2]): i for i, op in enumerate(SENDS)}
NSEM = len(SENDS)


def split(a):
    hi = a.astype(jnp.bfloat16)
    lo = (a - hi.astype(jnp.float32)).astype(jnp.bfloat16)
    return hi, lo


def dot3s(a, b):
    (ah, al), (bh, bl) = a, b
    d = lambda p, q: jnp.dot(p, q, preferred_element_type=jnp.float32)
    return d(ah, bh) + (d(ah, bl) + d(al, bh))


def dot3(a, b):
    return dot3s(split(a), split(b))


def gather_solve(f_ref, r_ref, g_ref, x_ref, top, cur, inv, ssem, rsem, xs, xr, ts, tr, tl, lsem, gate):
    src = lax.axis_index("src")
    row = lax.axis_index("row")
    z, h, x = src // (NH * NX), lax.rem(src // NX, NH), lax.rem(src, NX)
    core, y_lo = lax.rem(row, 2), row // 2

    def dev(dz=0, flip=False, dx=0):
        zz = lax.rem(z + dz + NZ, NZ)
        hh = 1 - h if flip else h
        return (zz * (NH * NX) + hh * NX + lax.rem(x + dx + NX, NX), row)

    link_to = {"x+": dev(dx=1), "x-": dev(dx=-1), "z+": dev(dz=1), "z-": dev(dz=-1), "y": dev(flip=True)}
    beside = (src, row + 1 - 2 * core)
    across = ((src, lax.rem(row + 2, 4)), (dev(flip=True)[0], lax.rem(row + 2, 4)))
    barrier = pltpu.get_barrier_semaphore()
    friends = list(link_to.values()) + [beside, *across]
    for friend in friends:
        pl.semaphore_signal(barrier, inc=1, device_id=friend, device_id_type=MESH)
    keep = pltpu.make_async_copy(f_ref, g_ref.at[z, h, x], lsem.at[0])
    keep.start()
    fetch = pltpu.make_async_copy(r_ref.at[pl.ds(0, COLS)], cur, lsem.at[1])
    first = jnp.logical_and(core == 0, y_lo == 0)
    pl.when(first)(fetch.start)
    pl.semaphore_wait(barrier, len(friends))

    def remote(a, b, s, r, to):
        return pltpu.make_async_remote_copy(
            src_ref=a, dst_ref=b, send_sem=s, recv_sem=r, device_id=to, device_id_type=MESH
        )

    ROWS = {"Y": (0, PIECE), "B1": (ROWS_A, PIECE - ROWS_A), "B3": (ROWS_A, PIECE - ROWS_A),
            "A1": (0, ROWS_A), "A3": (0, ROWS_A)}

    def where(tag):
        kind, dz, dh, dx = tag
        rows = pl.ds(*ROWS[kind])
        zz, hh = lax.rem(z + dz + NZ, NZ), h if dh == 0 else 1 - h
        return (zz, hh, slice(None), rows) if kind == "A3" else (zz, hh, lax.rem(x + dx + NX, NX), rows)

    def sent(i):
        _, link, tag = SENDS[i]
        b = g_ref.at[where(tag)]
        a = f_ref.at[pl.ds(*ROWS[tag[0]])] if tag[1:] == (0, 0, 0) and tag[0] != "A3" else b
        return remote(a, b, ssem.at[i], rsem.at[i], link_to[link])

    def landed(i):
        _, link, (kind, dz, dh, dx) = SENDS[i]
        step = {"+": 1, "-": -1}.get(link[-1], 0)
        if link[0] == "z":
            dz -= step
        elif link[0] == "x":
            dx -= step
        else:
            dh = 1 - dh
        return kind, dz, dh, dx

    handed = []

    def units(tag):
        kind, dz, dh, dx = tag
        start, n = ROWS[kind]
        zz, hh = lax.rem(z + dz + NZ, NZ), h if dh == 0 else 1 - h
        for e in range(NX) if kind == "A3" else (dx,):
            xx = e if kind == "A3" else lax.rem(x + dx + NX, NX)
            p = (zz * NH + hh) * NX + xx
            own = kind == "B3" and tag[1:] == (0, 0, 0)
            a = f_ref.at[pl.ds(start, n)] if own else g_ref.at[zz, hh, xx, pl.ds(start, n)]
            yield zz, lax.min(p, PIECES - 1), jnp.logical_and(first, p < PIECES), a, (0 if kind == "A3" else PIECES), (start, n)

    def copies(tag):
        for zz, p, go, a, base, (start, n) in units(tag):
            b = top.at[pl.ds(p * PIECE + start, n)]
            yield go, pltpu.make_async_copy(a, b, tl.at[base + p]), False
            if tag[2] == 0:
                yield jnp.logical_and(go, zz >= 1), remote(a, b, ts.at[base + p], tr.at[base + p], across[0]), True
                yield go, remote(a, b, ts.at[UNITS + base + p], tr.at[base + p], across[1]), True
            else:
                yield jnp.logical_and(go, zz == 0), remote(a, b, ts.at[UNITS + base + p], tr.at[base + p], across[1]), True

    def hand_up(tag):
        for go, c, _ in copies(tag):
            pl.when(go)(c.start)
        handed.append(tag)

    def right(i):
        rows = pl.ds(i * (COLS // CHUNKS), COLS // CHUNKS)
        return remote(r_ref.at[rows], cur.at[rows], ts.at[2 * UNITS + i], tr.at[UNITS + i], across[0])

    @pl.when(core == 1)
    def _():
        pl.semaphore_wait(gate, 1)

    kept = False
    arrived = 0
    for op, link, tag in ORDER:
        i = SEND_INDEX[(link, tag)]
        if op == "send":
            if tag[0] == "A3" and not kept:
                keep.wait()
                kept = True
            sent(i).start()
            if link == "z+" and tag[1] == 0:
                if tag[0] == "A3":
                    hand_up(("A3", 0, tag[2], 0))
                elif tag[2] == 1:
                    hand_up(("B3", 0, 0, 0))
                    hand_up(("B3", 0, 1, 0))
            continue
        got = landed(i)
        b = g_ref.at[where(got)]
        remote(b, b, ssem.at[i], rsem.at[i], link_to[link]).wait_recv()
        if got[0] in ("A3", "B3"):
            hand_up(got)
        elif got[0] == "B1":
            hand_up(("B3",) + got[1:])
        arrived += 1
        if arrived == GATE:
            @pl.when(core == 0)
            def _():
                pl.semaphore_signal(gate, inc=1, device_id=beside, device_id_type=MESH)

        if arrived % 12 == 11 and arrived // 12 < CHUNKS:
            pl.when(first)(right(arrived // 12).start)

    def x_send(j):
        rows = pl.ds(j * BLK, BLK)
        return remote(cur.at[rows], x_ref.at[rows], xs.at[j], xr.at[j], beside)

    @pl.when(core == 0)
    def _():
        def part(p, base):
            start, n = ROWS["A3"] if base == 0 else ROWS["B3"]
            return top.at[pl.ds(p * PIECE + start, n)]

        @pl.when(y_lo == 0)
        def _():
            for base in (0, PIECES):
                for p in range(PIECES):
                    pltpu.make_async_copy(part(p, base), part(p, base), tl.at[base + p]).wait()
            fetch.wait()

        @pl.when(y_lo == 1)
        def _():
            for base in (0, PIECES):
                for p in range(PIECES):
                    remote(part(p, base), part(p, base), ts.at[base + p], tr.at[base + p], across[0]).wait_recv()
            for i in range(CHUNKS):
                right(i).wait_recv()

        ii = lax.broadcasted_iota(jnp.int32, (BLK, BLK), 0)
        jj = lax.broadcasted_iota(jnp.int32, (BLK, BLK), 1)
        for j in range(STEPS):
            a = top[pl.ds(j * BLK, BLK), pl.ds(j * BLK, BLK)]
            dg = jnp.where(ii == jj, a, 0.0)
            dc = 1.0 / jnp.sum(dg, axis=1, keepdims=True)
            dr = 1.0 / jnp.sum(dg, axis=0, keepdims=True)
            pair = jnp.logical_and(ii == jj + 1, lax.rem(ii, 2) == 1)
            inv[j] = jnp.where(ii == jj, dc, jnp.where(pair, -(dc * a) * dr, 0.0))

        def level(t, carry):
            bi, bj = lax.shift_right_logical(ii, t), lax.shift_right_logical(jj, t)
            below = jnp.logical_and(bi == bj + 1, lax.rem(bi, 2) == 1)
            v = [split(inv[j]) for j in range(STEPS)]
            e = [split(jnp.where(below, top[pl.ds(j * BLK, BLK), pl.ds(j * BLK, BLK)], 0.0)) for j in range(STEPS)]
            w = [split(dot3s(e[j], v[j])) for j in range(STEPS)]
            w = [dot3s(v[j], w[j]) for j in range(STEPS)]
            for j in range(STEPS):
                inv[j] = inv[j] - w[j]
            return carry

        lax.fori_loop(1, 7, level, 0)
        for j in range(STEPS):
            rows = pl.ds(j * BLK, BLK)
            solved = dot3(inv[j], cur[rows])
            cur[rows] = solved
            left = COLS - (j + 1) * BLK
            if left:
                below = pl.ds((j + 1) * BLK, left)
                cur[below] = cur[below] - dot3(top[below, rows], solved)
            if j >= 1:
                x_send(j - 1).start()
        store = pltpu.make_async_copy(cur, x_ref, lsem.at[2])
        store.start()
        x_send(STEPS - 1).start()
        store.wait()
        for j in range(STEPS):
            x_send(j).wait_send()

    @pl.when(core == 1)
    def _():
        for j in range(STEPS):
            x_send(j).wait_recv()

    for i in range(NSEM):
        sent(i).wait_send()
    for tag in handed:
        for go, c, away in copies(tag):
            if away:
                pl.when(go)(c.wait_send)

    @pl.when(first)
    def _():
        for i in range(CHUNKS):
            right(i).wait_send()


TILE = 512


def update(f_ref, x_ref, r_ref, o_ref, fb, rb, ob, xb, xh, xl, sems):
    row = lax.axis_index("row")
    n = f_ref.shape[0] // TILE
    tile = lambda i: pl.ds(i * TILE, TILE)
    get_x = pltpu.make_async_copy(x_ref, xb, sems.at[0])
    get_f = [pltpu.make_async_copy(f_ref.at[tile(i)], fb.at[tile(i)], sems.at[1 + i]) for i in range(n)]
    get_r = [pltpu.make_async_copy(r_ref.at[tile(i)], rb.at[tile(i)], sems.at[1 + n + i]) for i in range(n)]
    put = [pltpu.make_async_copy(ob.at[tile(i)], o_ref.at[tile(i)], sems.at[1 + 2 * n + i]) for i in range(n)]
    get_x.start()
    for f, r in zip(get_f, get_r):
        f.start()
        r.start()
    get_x.wait()
    hi, lo = split(xb[...])
    xh[...] = hi
    xl[...] = lo

    def advance(i):
        fh, fl = split(fb[tile(i)])
        d = lambda p, q: jnp.dot(p, q[...], preferred_element_type=jnp.float32)
        ob[tile(i)] = rb[tile(i)] - (d(fh, xh) + (d(fh, xl) + d(fl, xh)))

    for i in range(n):
        get_f[i].wait()
        get_r[i].wait()
        if i < COLS // TILE:
            @pl.when(row == 0)
            def _():
                ob[tile(i)] = xb[tile(i)]

            @pl.when(row != 0)
            def _():
                advance(i)
        else:
            advance(i)
        put[i].start()
    for c in put:
        c.wait()


def local(factor, right_side):
    rows, width = right_side.shape
    ANY = pl.BlockSpec(memory_space=pl.ANY)
    gathered, solved = pl.pallas_call(
        gather_solve,
        out_shape=(
            jax.ShapeDtypeStruct((NZ, NH, NX, PIECE, COLS), jnp.float32),
            jax.ShapeDtypeStruct((COLS, width), jnp.float32),
        ),
        in_specs=[pl.BlockSpec(memory_space=pltpu.VMEM), ANY],
        out_specs=(ANY, ANY),
        scratch_shapes=[
            pltpu.VMEM((PIECES * PIECE, COLS), jnp.float32),
            pltpu.VMEM((COLS, width), jnp.float32),
            pltpu.VMEM((STEPS, BLK, BLK), jnp.float32),
            pltpu.SemaphoreType.DMA((NSEM,)),
            pltpu.SemaphoreType.DMA((NSEM,)),
            pltpu.SemaphoreType.DMA((STEPS,)),
            pltpu.SemaphoreType.DMA((STEPS,)),
            pltpu.SemaphoreType.DMA((2 * UNITS + CHUNKS,)),
            pltpu.SemaphoreType.DMA((UNITS + CHUNKS,)),
            pltpu.SemaphoreType.DMA((UNITS,)),
            pltpu.SemaphoreType.DMA((3,)),
            pltpu.SemaphoreType.REGULAR,
        ],
        compiler_params=pltpu.CompilerParams(collective_id=0, has_side_effects=True),
    )(factor, right_side)
    return pl.pallas_call(
        update,
        out_shape=jax.ShapeDtypeStruct((rows, width), jnp.float32),
        in_specs=[ANY, ANY, ANY],
        out_specs=ANY,
        scratch_shapes=[
            pltpu.VMEM((rows, COLS), jnp.float32),
            pltpu.VMEM((rows, width), jnp.float32),
            pltpu.VMEM((rows, width), jnp.float32),
            pltpu.VMEM((COLS, width), jnp.float32),
            pltpu.VMEM((COLS, width), jnp.bfloat16),
            pltpu.VMEM((COLS, width), jnp.bfloat16),
            pltpu.SemaphoreType.DMA((3 * rows // TILE + 1,)),
        ],
    )(gathered.reshape(rows, COLS), solved, right_side)


def solution(mesh):
    placed = (P(("row", "src"), None), P("row", "src"))
    return jax.shard_map(
        local, mesh=mesh, in_specs=placed, out_specs=P("row", "src"), check_vma=False
    )
```

```python
import heapq

import jax
import jax.numpy as jnp
from jax import lax
from jax.experimental import pallas as pl
from jax.experimental.pallas import tpu as pltpu
from jax.sharding import PartitionSpec as P

MESH = pl.DeviceIdType.MESH
NX, NH, NZ = 4, 2, 8
PIECE = 40
COLS = 1024
WIDTH = 512
BLK = 128
STEPS = COLS // BLK
PIECES = -(-COLS // PIECE)
UNITS = 2 * PIECES
CHUNKS = 4
GATE = 36
RATE = {"x+": 70e3, "x-": 70e3, "z+": 70e3, "z-": 70e3, "y": 60e3}


def plan(rows_a, latency=1.7):
    size = {"Y": PIECE, "B1": PIECE - rows_a, "B3": PIECE - rows_a, "A1": rows_a, "A3": 4 * rows_a}
    free = dict.fromkeys(RATE, 0.0)
    heap, order = [], []

    def send(t, link, tag):
        end = max(t, free[link]) + size[tag[0]] * 4096 / RATE[link]
        free[link] = end
        heapq.heappush(heap, (end + latency, len(order), link, tag))
        order.append(("send", link, tag))

    def own(t, dh):
        for link in ("z+", "z-"):
            send(t, link, ("B1", 0, dh, 0))
        for link in ("x+", "x-"):
            send(t, link, ("A1", 0, dh, 0))
        for link in ("x+", "x-"):
            send(t, link, ("B3", 0, dh, 0))

    send(0, "y", ("Y", 0, 0, 0))
    own(0, 0)
    got = {0: 0, 1: 0}
    while heap:
        t, _, link, tag = heapq.heappop(heap)
        kind, dz, dh, dx = tag
        step = {"+": 1, "-": -1}.get(link[-1], 0)
        order.append(("recv", link, tag))
        if kind == "Y":
            own(t, 1)
            continue
        if link[0] == "x":
            dx -= step
        else:
            dz -= step
        if kind in ("B1", "A3"):
            far = abs(dz) + 1
            if far <= 3 or (far == 4 and (dh == 0) == (step == 1)):
                send(t, link, (kind, dz, dh, dx))
            if kind == "B1":
                for side in ("x+", "x-"):
                    send(t, side, ("B3", dz, dh, 0))
        else:
            if abs(dx) == 1 and (dh == 0) == (step == 1):
                send(t, link, (kind, dz, dh, dx))
            if kind == "A1":
                got[dh] += 1
                if got[dh] == 3:
                    for side in ("z+", "z-"):
                        send(t, side, ("A3", 0, dh, 0))
    return order


ROWS_A = 16
ORDER = plan(ROWS_A)
SENDS = [op for op in ORDER if op[0] == "send"]
SEND_INDEX = {(op[1], op[2]): i for i, op in enumerate(SENDS)}
NSEM = len(SENDS)


def split(a):
    hi = a.astype(jnp.bfloat16)
    lo = (a - hi.astype(jnp.float32)).astype(jnp.bfloat16)
    return hi, lo


def dot3s(a, b):
    (ah, al), (bh, bl) = a, b
    d = lambda p, q: jnp.dot(p, q, preferred_element_type=jnp.float32)
    return d(ah, bh) + (d(ah, bl) + d(al, bh))


def dot3(a, b):
    return dot3s(split(a), split(b))


def gather_solve(f_ref, r_ref, g_ref, x_ref, top, cur, inv, ssem, rsem, xs, xr, ts, tr, tl, lsem, gate):
    src = lax.axis_index("src")
    row = lax.axis_index("row")
    z, h, x = src // (NH * NX), lax.rem(src // NX, NH), lax.rem(src, NX)
    core, y_lo = lax.rem(row, 2), row // 2

    def dev(dz=0, flip=False, dx=0):
        zz = lax.rem(z + dz + NZ, NZ)
        hh = 1 - h if flip else h
        return (zz * (NH * NX) + hh * NX + lax.rem(x + dx + NX, NX), row)

    link_to = {"x+": dev(dx=1), "x-": dev(dx=-1), "z+": dev(dz=1), "z-": dev(dz=-1), "y": dev(flip=True)}
    beside = (src, row + 1 - 2 * core)
    across = ((src, lax.rem(row + 2, 4)), (dev(flip=True)[0], lax.rem(row + 2, 4)))
    barrier = pltpu.get_barrier_semaphore()
    friends = list(link_to.values()) + [beside, *across]
    for friend in friends:
        pl.semaphore_signal(barrier, inc=1, device_id=friend, device_id_type=MESH)
    keep = pltpu.make_async_copy(f_ref, g_ref.at[z, h, x], lsem.at[0])
    keep.start()
    fetch = pltpu.make_async_copy(r_ref.at[pl.ds(0, COLS)], cur, lsem.at[1])
    first = jnp.logical_and(core == 0, y_lo == 0)
    pl.when(first)(fetch.start)
    pl.semaphore_wait(barrier, len(friends))

    def remote(a, b, s, r, to):
        return pltpu.make_async_remote_copy(
            src_ref=a, dst_ref=b, send_sem=s, recv_sem=r, device_id=to, device_id_type=MESH
        )

    ROWS = {"Y": (0, PIECE), "B1": (ROWS_A, PIECE - ROWS_A), "B3": (ROWS_A, PIECE - ROWS_A),
            "A1": (0, ROWS_A), "A3": (0, ROWS_A)}

    def where(tag):
        kind, dz, dh, dx = tag
        rows = pl.ds(*ROWS[kind])
        zz, hh = lax.rem(z + dz + NZ, NZ), h if dh == 0 else 1 - h
        return (zz, hh, slice(None), rows) if kind == "A3" else (zz, hh, lax.rem(x + dx + NX, NX), rows)

    def sent(i):
        _, link, tag = SENDS[i]
        b = g_ref.at[where(tag)]
        a = f_ref.at[pl.ds(*ROWS[tag[0]])] if tag[1:] == (0, 0, 0) and tag[0] != "A3" else b
        return remote(a, b, ssem.at[i], rsem.at[i], link_to[link])

    def landed(i):
        _, link, (kind, dz, dh, dx) = SENDS[i]
        step = {"+": 1, "-": -1}.get(link[-1], 0)
        if link[0] == "z":
            dz -= step
        elif link[0] == "x":
            dx -= step
        else:
            dh = 1 - dh
        return kind, dz, dh, dx

    handed = []

    def units(tag):
        kind, dz, dh, dx = tag
        start, n = ROWS[kind]
        zz, hh = lax.rem(z + dz + NZ, NZ), h if dh == 0 else 1 - h
        for e in range(NX) if kind == "A3" else (dx,):
            xx = e if kind == "A3" else lax.rem(x + dx + NX, NX)
            p = (zz * NH + hh) * NX + xx
            own = kind == "B3" and tag[1:] == (0, 0, 0)
            a = f_ref.at[pl.ds(start, n)] if own else g_ref.at[zz, hh, xx, pl.ds(start, n)]
            yield zz, lax.min(p, PIECES - 1), jnp.logical_and(first, p < PIECES), a, (0 if kind == "A3" else PIECES), (start, n)

    def copies(tag):
        for zz, p, go, a, base, (start, n) in units(tag):
            b = top.at[pl.ds(p * PIECE + start, n)]
            yield go, pltpu.make_async_copy(a, b, tl.at[base + p]), False
            early = abs(tag[1]) <= 1
            if tag[2] == 0:
                if not early:
                    yield go, remote(a, b, ts.at[base + p], tr.at[base + p], across[0]), True
                yield go, remote(a, b, ts.at[UNITS + base + p], tr.at[base + p], across[1]), True
            elif early:
                yield go, remote(a, b, ts.at[UNITS + base + p], tr.at[base + p], across[1]), True

    def hand_up(tag):
        for go, c, _ in copies(tag):
            pl.when(go)(c.start)
        handed.append(tag)

    def right(i):
        rows = pl.ds(i * (COLS // CHUNKS), COLS // CHUNKS)
        return remote(r_ref.at[rows], cur.at[rows], ts.at[2 * UNITS + i], tr.at[UNITS + i], across[0])

    @pl.when(core == 1)
    def _():
        pl.semaphore_wait(gate, 1)

    kept = False
    arrived = 0
    for op, link, tag in ORDER:
        i = SEND_INDEX[(link, tag)]
        if op == "send":
            if tag[0] == "A3" and not kept:
                keep.wait()
                kept = True
            sent(i).start()
            if link == "z+" and tag[1] == 0:
                if tag[0] == "A3":
                    hand_up(("A3", 0, tag[2], 0))
                elif tag[2] == 1:
                    hand_up(("B3", 0, 0, 0))
                    hand_up(("B3", 0, 1, 0))
            continue
        got = landed(i)
        b = g_ref.at[where(got)]
        remote(b, b, ssem.at[i], rsem.at[i], link_to[link]).wait_recv()
        if got[0] in ("A3", "B3"):
            hand_up(got)
        elif got[0] == "B1":
            hand_up(("B3",) + got[1:])
        arrived += 1
        if arrived == GATE:
            @pl.when(core == 0)
            def _():
                pl.semaphore_signal(gate, inc=1, device_id=beside, device_id_type=MESH)

        if arrived % 12 == 11 and arrived // 12 < CHUNKS:
            pl.when(first)(right(arrived // 12).start)

    def x_send(j):
        rows = pl.ds(j * BLK, BLK)
        return remote(cur.at[rows], x_ref.at[rows], xs.at[j], xr.at[j], beside)

    @pl.when(core == 0)
    def _():
        def part(p, base):
            start, n = ROWS["A3"] if base == 0 else ROWS["B3"]
            return top.at[pl.ds(p * PIECE + start, n)]

        @pl.when(y_lo == 0)
        def _():
            for base in (0, PIECES):
                for p in range(PIECES):
                    pltpu.make_async_copy(part(p, base), part(p, base), tl.at[base + p]).wait()
            fetch.wait()

        @pl.when(y_lo == 1)
        def _():
            for base in (0, PIECES):
                for p in range(PIECES):
                    remote(part(p, base), part(p, base), ts.at[base + p], tr.at[base + p], across[0]).wait_recv()
            for i in range(CHUNKS):
                right(i).wait_recv()

        ii = lax.broadcasted_iota(jnp.int32, (BLK, BLK), 0)
        jj = lax.broadcasted_iota(jnp.int32, (BLK, BLK), 1)
        for j in range(STEPS):
            a = top[pl.ds(j * BLK, BLK), pl.ds(j * BLK, BLK)]
            dg = jnp.where(ii == jj, a, 0.0)
            dc = 1.0 / jnp.sum(dg, axis=1, keepdims=True)
            dr = 1.0 / jnp.sum(dg, axis=0, keepdims=True)
            pair = jnp.logical_and(ii == jj + 1, lax.rem(ii, 2) == 1)
            inv[j] = jnp.where(ii == jj, dc, jnp.where(pair, -(dc * a) * dr, 0.0))

        def level(t, carry):
            bi, bj = lax.shift_right_logical(ii, t), lax.shift_right_logical(jj, t)
            below = jnp.logical_and(bi == bj + 1, lax.rem(bi, 2) == 1)
            v = [split(inv[j]) for j in range(STEPS)]
            e = [split(jnp.where(below, top[pl.ds(j * BLK, BLK), pl.ds(j * BLK, BLK)], 0.0)) for j in range(STEPS)]
            w = [split(dot3s(e[j], v[j])) for j in range(STEPS)]
            w = [dot3s(v[j], w[j]) for j in range(STEPS)]
            for j in range(STEPS):
                inv[j] = inv[j] - w[j]
            return carry

        lax.fori_loop(1, 7, level, 0)
        for j in range(STEPS):
            rows = pl.ds(j * BLK, BLK)
            solved = dot3(inv[j], cur[rows])
            cur[rows] = solved
            left = COLS - (j + 1) * BLK
            if left:
                below = pl.ds((j + 1) * BLK, left)
                cur[below] = cur[below] - dot3(top[below, rows], solved)
            if j >= 1:
                x_send(j - 1).start()
        store = pltpu.make_async_copy(cur, x_ref, lsem.at[2])
        store.start()
        x_send(STEPS - 1).start()
        store.wait()
        for j in range(STEPS):
            x_send(j).wait_send()

    @pl.when(core == 1)
    def _():
        for j in range(STEPS):
            x_send(j).wait_recv()

    for i in range(NSEM):
        sent(i).wait_send()
    for tag in handed:
        for go, c, away in copies(tag):
            if away:
                pl.when(go)(c.wait_send)

    @pl.when(first)
    def _():
        for i in range(CHUNKS):
            right(i).wait_send()


TILE = 512


def update(f_ref, x_ref, r_ref, o_ref, fb, rb, ob, xb, xh, xl, sems):
    row = lax.axis_index("row")
    n = f_ref.shape[0] // TILE
    tile = lambda i: pl.ds(i * TILE, TILE)
    get_x = pltpu.make_async_copy(x_ref, xb, sems.at[0])
    get_f = [pltpu.make_async_copy(f_ref.at[tile(i)], fb.at[tile(i)], sems.at[1 + i]) for i in range(n)]
    get_r = [pltpu.make_async_copy(r_ref.at[tile(i)], rb.at[tile(i)], sems.at[1 + n + i]) for i in range(n)]
    put = [pltpu.make_async_copy(ob.at[tile(i)], o_ref.at[tile(i)], sems.at[1 + 2 * n + i]) for i in range(n)]
    get_x.start()
    for f, r in zip(get_f, get_r):
        f.start()
        r.start()
    get_x.wait()
    hi, lo = split(xb[...])
    xh[...] = hi
    xl[...] = lo

    def advance(i):
        fh, fl = split(fb[tile(i)])
        d = lambda p, q: jnp.dot(p, q[...], preferred_element_type=jnp.float32)
        ob[tile(i)] = rb[tile(i)] - (d(fh, xh) + (d(fh, xl) + d(fl, xh)))

    for i in range(n):
        get_f[i].wait()
        get_r[i].wait()
        if i < COLS // TILE:
            @pl.when(row == 0)
            def _():
                ob[tile(i)] = xb[tile(i)]

            @pl.when(row != 0)
            def _():
                advance(i)
        else:
            advance(i)
        put[i].start()
    for c in put:
        c.wait()


def local(factor, right_side):
    rows, width = right_side.shape
    ANY = pl.BlockSpec(memory_space=pl.ANY)
    gathered, solved = pl.pallas_call(
        gather_solve,
        out_shape=(
            jax.ShapeDtypeStruct((NZ, NH, NX, PIECE, COLS), jnp.float32),
            jax.ShapeDtypeStruct((COLS, width), jnp.float32),
        ),
        in_specs=[pl.BlockSpec(memory_space=pltpu.VMEM), ANY],
        out_specs=(ANY, ANY),
        scratch_shapes=[
            pltpu.VMEM((PIECES * PIECE, COLS), jnp.float32),
            pltpu.VMEM((COLS, width), jnp.float32),
            pltpu.VMEM((STEPS, BLK, BLK), jnp.float32),
            pltpu.SemaphoreType.DMA((NSEM,)),
            pltpu.SemaphoreType.DMA((NSEM,)),
            pltpu.SemaphoreType.DMA((STEPS,)),
            pltpu.SemaphoreType.DMA((STEPS,)),
            pltpu.SemaphoreType.DMA((2 * UNITS + CHUNKS,)),
            pltpu.SemaphoreType.DMA((UNITS + CHUNKS,)),
            pltpu.SemaphoreType.DMA((UNITS,)),
            pltpu.SemaphoreType.DMA((3,)),
            pltpu.SemaphoreType.REGULAR,
        ],
        compiler_params=pltpu.CompilerParams(collective_id=0, has_side_effects=True),
    )(factor, right_side)
    return pl.pallas_call(
        update,
        out_shape=jax.ShapeDtypeStruct((rows, width), jnp.float32),
        in_specs=[ANY, ANY, ANY],
        out_specs=ANY,
        scratch_shapes=[
            pltpu.VMEM((rows, COLS), jnp.float32),
            pltpu.VMEM((rows, width), jnp.float32),
            pltpu.VMEM((rows, width), jnp.float32),
            pltpu.VMEM((COLS, width), jnp.float32),
            pltpu.VMEM((COLS, width), jnp.bfloat16),
            pltpu.VMEM((COLS, width), jnp.bfloat16),
            pltpu.SemaphoreType.DMA((3 * rows // TILE + 1,)),
        ],
    )(gathered.reshape(rows, COLS), solved, right_side)


def solution(mesh):
    placed = (P(("row", "src"), None), P("row", "src"))
    return jax.shard_map(
        local, mesh=mesh, in_specs=placed, out_specs=P("row", "src"), check_vma=False
    )
```
